512 devices in a mesh: head: 32 (over y, z_lo), seq: 8 (over x, core), batch: 2 (over z_hi).
Axes of the slice: x: 4, y: 8, z: 8 (z_hi: 2, z_lo: 4; z = z_hi * 4 + z_lo), core: 2. Of those that a mesh axis runs over, the one named last changes fastest.
Arguments:
- teacher_qkv: bfloat16 [1, 128, 512, 8192], P(None, ('seq', 'batch'), None, 'head'), may hold values from -24 to 24
- student_qkv: bfloat16 [1, 128, 512, 4096], P(None, ('seq', 'batch'), 'head'), may hold values from -24 to 24
Outputs:
- student_grads: bfloat16 [1, 128, 512, 4096], P(None, ('seq', 'batch'), 'head')
The draws below stay inside these ranges and needn't reach their ends.
All inputs are finite; a program needn't handle non-finite values.
Results may differ from the reference program's by a relative error of at most 0.0045.
Values may be sent and summed in bfloat16 or wider, within the bound.
A program may use at most 64 MiB of HBM per device.

```python
import math
import jax
import jax.numpy as jnp
from jax import lax

TEACHER_WIDTH = 8192
STUDENT_WIDTH = 4096
RELATION_HEADS = 64
KINDS = 1
LENGTH = 512
BATCH = 128


def draw_features(key, width):
    base_key = jax.random.fold_in(key, 11)
    scale_key = jax.random.fold_in(key, 12)
    shape = (KINDS, BATCH, LENGTH, width)
    entries = jnp.clip(jax.random.normal(base_key, shape, jnp.float32), -4.5, 4.5)
    row_scale = jnp.exp(jax.random.uniform(scale_key, (KINDS, BATCH, LENGTH, 1), jnp.float32, math.log(0.6), math.log(1.4)))
    values = 0.85 * entries * row_scale
    return jnp.clip(values, -24.0, 24.0)


def draw_teacher_qkv(key, part):
    return draw_features(jax.random.fold_in(key, 1), TEACHER_WIDTH).astype(jnp.bfloat16)


def draw_student_qkv(key, part):
    return draw_features(jax.random.fold_in(key, 2), STUDENT_WIDTH).astype(jnp.bfloat16)


def setup_inputs(seed: int = 0) -> dict:
    splits = jax.random.split(jax.random.key(seed), 3)
    teacher_qkv = draw_teacher_qkv(jax.random.fold_in(splits[2], 71), 0)
    student_qkv = draw_student_qkv(jax.random.fold_in(splits[2], 71), 0)
    return {"teacher_qkv": teacher_qkv, "student_qkv": student_qkv}


def reference(teacher_qkv, student_qkv):
    teacher_width = TEACHER_WIDTH // RELATION_HEADS
    student_width = STUDENT_WIDTH // RELATION_HEADS
    teacher_factor = 1.0 / math.sqrt(teacher_width)
    student_factor = 1.0 / math.sqrt(student_width)

    def softmax_rows(scores):
        row_peak = lax.optimization_barrier(jnp.max(scores, axis=1, keepdims=True))
        weights = jnp.exp(scores - row_peak)
        return weights / lax.optimization_barrier(jnp.sum(weights, axis=1, keepdims=True))

    def head_gradient(operands):
        teacher_part, student_part = operands
        teacher_scores = jnp.dot(teacher_part, teacher_part.T, precision=lax.Precision.HIGHEST) * teacher_factor
        student_scores = jnp.dot(student_part, student_part.T, precision=lax.Precision.HIGHEST) * student_factor
        difference = (softmax_rows(student_scores) - softmax_rows(teacher_scores)).astype(jnp.bfloat16)
        difference = lax.optimization_barrier(difference).astype(jnp.float32)
        query_side = jnp.dot(difference, student_part, precision=lax.Precision.HIGHEST)
        key_side = jnp.dot(difference.T, student_part, precision=lax.Precision.HIGHEST)
        return ((query_side + key_side) * student_factor).astype(jnp.bfloat16)

    def sequence_gradient(operands):
        teacher_rows, student_rows = operands
        teacher_heads = teacher_rows.astype(jnp.float32).reshape(LENGTH, RELATION_HEADS, teacher_width).transpose(1, 0, 2)
        student_heads = student_rows.astype(jnp.float32).reshape(LENGTH, RELATION_HEADS, student_width).transpose(1, 0, 2)
        gradients = lax.map(head_gradient, (teacher_heads, student_heads))
        return gradients.transpose(1, 0, 2).reshape(LENGTH, STUDENT_WIDTH)
    teacher_flat = teacher_qkv.reshape(KINDS * BATCH, LENGTH, TEACHER_WIDTH)
    student_flat = student_qkv.reshape(KINDS * BATCH, LENGTH, STUDENT_WIDTH)
    results = lax.map(sequence_gradient, (teacher_flat, student_flat))
    return results.reshape(KINDS, BATCH, LENGTH, STUDENT_WIDTH)
```

```python
import functools
import math

import jax
import jax.numpy as jnp
from jax import lax
from jax.experimental import pallas as pl
from jax.experimental.pallas import tpu as pltpu
from jax.sharding import PartitionSpec as P

RELATION_HEADS = 64
CHUNK = 2
STRIP = 256
LOG2E = 1.4426950408889634
F32, BF16 = jnp.float32, jnp.bfloat16
MESH = pl.DeviceIdType.MESH
NT = (((1,), (1,)), ((), ()))


def probs(rows, some, factor):
    scores = lax.dot_general(rows, some, NT, preferred_element_type=F32)
    peak = jnp.max(scores, axis=0, keepdims=True)
    weights = jnp.exp2((scores - peak) * factor)
    return weights * (1.0 / jnp.sum(weights, axis=0, keepdims=True))


def item_gradient(heads, teacher, student, grads, diff):
    length = teacher.shape[0]
    tw, sw = teacher.shape[1] // heads, student.shape[1] // heads
    x = student[...]
    lane = lax.broadcasted_iota(jnp.int32, x.shape, 1)
    x_t = x.T
    parts = []
    for head in range(heads):
        mine = (lane >= head * sw) & (lane < (head + 1) * sw)
        xh = jnp.where(mine, x, jnp.zeros_like(x))
        th = teacher[:, head * tw : (head + 1) * tw]
        for i in range(0, length, STRIP):
            student_probs = probs(x, xh[i : i + STRIP], LOG2E / math.sqrt(sw))
            teacher_probs = probs(th, th[i : i + STRIP], LOG2E / math.sqrt(tw))
            diff[:, i : i + STRIP] = (student_probs - teacher_probs).astype(BF16)
        xh_t = x_t[head * sw : (head + 1) * sw]
        d = diff[...]
        key_side = lax.dot_general(xh_t, d, NT, preferred_element_type=F32)
        query_side = jnp.dot(xh_t, d, preferred_element_type=F32)
        parts.append(query_side + key_side)
    grads_t = jnp.concatenate(parts, axis=0) * (1.0 / math.sqrt(sw))
    grads[...] = grads_t.T.astype(BF16)


def kernel(ny, nz, heads, teacher_hbm, student_hbm, out, teacher, staged, xs, grads, diff, sems, in_recv, t_sem):
    n = ny * nz
    me = lax.axis_index("head")
    y, z = me // nz, me % nz
    items, rows, _ = staged.shape
    width = xs.shape[2]
    load_sem, in_send, out_send, out_recv = (sems.at[i] for i in range(4))

    def peer(t):
        a, dz = t // nz, t % nz
        dy = (a % 2) * ((a + 1) // 2) + (1 - a % 2) * (ny - a // 2)
        return ((y + dy) % ny) * nz + (z + dz) % nz

    load = pltpu.make_async_copy(student_hbm, staged, load_sem)
    load.start()

    def load_teacher(b, _):
        pltpu.make_async_copy(teacher_hbm.at[b], teacher.at[b], t_sem.at[b]).start()
        return 0

    lax.fori_loop(0, items, load_teacher, 0)

    barrier = pltpu.get_barrier_semaphore()

    def greet(t, _):
        pl.semaphore_signal(barrier, inc=1, device_id={"head": peer(t)}, device_id_type=MESH)
        return 0

    lax.fori_loop(1, n, greet, 0)
    load.wait()
    pl.semaphore_wait(barrier, n - 1)

    my_rows = pl.ds(pl.multiple_of(me * rows, rows), rows)
    my_cols = pl.ds(pl.multiple_of(me * width, width), width)

    def send_in(c, _):
        batch = pl.ds(c * CHUNK, CHUNK)
        pltpu.make_async_copy(
            staged.at[batch, :, my_cols], xs.at[batch, my_rows, :], in_recv.at[c]
        ).start()

        def to(t, _):
            p = peer(t)
            pltpu.make_async_remote_copy(
                src_ref=staged.at[batch, :, pl.ds(pl.multiple_of(p * width, width), width)],
                dst_ref=xs.at[batch, my_rows, :],
                send_sem=in_send,
                recv_sem=in_recv.at[c],
                device_id={"head": p},
                device_id_type=MESH,
            ).start()
            return 0

        lax.fori_loop(1, n, to, 0)
        return 0

    lax.fori_loop(0, items // CHUNK, send_in, 0)

    def work(c, _):
        batch = pl.ds(c * CHUNK, CHUNK)
        pltpu.make_async_copy(xs.at[batch], xs.at[batch], in_recv.at[c]).wait()
        for k in range(CHUNK):
            b = c * CHUNK + k
            pltpu.make_async_copy(teacher_hbm.at[b], teacher.at[b], t_sem.at[b]).wait()
            item_gradient(heads, teacher.at[b], xs.at[b], grads.at[b], diff)
        pltpu.make_async_copy(
            grads.at[batch, my_rows, :], out.at[batch, :, my_cols], out_recv
        ).start()

        def to(t, _):
            p = peer(t)
            pltpu.make_async_remote_copy(
                src_ref=grads.at[batch, pl.ds(pl.multiple_of(p * rows, rows), rows), :],
                dst_ref=out.at[batch, :, my_cols],
                send_sem=out_send,
                recv_sem=out_recv,
                device_id={"head": p},
                device_id_type=MESH,
            ).start()
            return 0

        lax.fori_loop(1, n, to, 0)
        return 0

    lax.fori_loop(0, items // CHUNK, work, 0)

    some = pl.ds(0, (n - 1) * rows)
    pltpu.make_async_copy(xs.at[:, some, :], xs.at[:, some, :], in_send).wait()
    pltpu.make_async_copy(grads.at[:, some, :], grads.at[:, some, :], out_send).wait()
    pltpu.make_async_copy(out, out, out_recv).wait()


def solution(mesh):
    n = mesh.shape["head"]
    nz = 4
    heads = RELATION_HEADS // n

    def body(teacher_qkv, student_qkv):
        _, items, length, teacher_width = teacher_qkv.shape
        _, _, rows, student_width = student_qkv.shape
        width = student_width // n
        result = pl.pallas_call(
            functools.partial(kernel, n // nz, nz, heads),
            out_shape=jax.ShapeDtypeStruct((items, rows, student_width), BF16),
            in_specs=[pl.BlockSpec(memory_space=pltpu.HBM)] * 2,
            out_specs=pl.BlockSpec(memory_space=pl.ANY),
            scratch_shapes=[
                pltpu.VMEM((items, length, teacher_width), BF16),
                pltpu.VMEM((items, rows, student_width), BF16),
                pltpu.VMEM((items, length, width), BF16),
                pltpu.VMEM((items, length, width), BF16),
                pltpu.VMEM((length, length), BF16),
                pltpu.SemaphoreType.DMA((4,)),
                pltpu.SemaphoreType.DMA((items // CHUNK,)),
                pltpu.SemaphoreType.DMA((items,)),
            ],
            compiler_params=pltpu.CompilerParams(
                collective_id=0, has_side_effects=True, vmem_limit_bytes=24 * 2**20
            ),
            name="relation_grads",
        )(teacher_qkv[0], student_qkv[0])
        return result[None]

    in_specs = (P(None, ("seq", "batch"), None, "head"), P(None, ("seq", "batch"), "head", None))
    out_specs = P(None, ("seq", "batch"), "head", None)
    return jax.shard_map(body, mesh=mesh, in_specs=in_specs, out_specs=out_specs, check_vma=False)
```

```python
import functools
import math

import jax
import jax.numpy as jnp
from jax import lax
from jax.experimental import pallas as pl
from jax.experimental.pallas import tpu as pltpu
from jax.sharding import PartitionSpec as P

RELATION_HEADS = 64
CHUNK = 2
STRIP = 256
EARLY = 3
LOG2E = 1.4426950408889634
F32, BF16 = jnp.float32, jnp.bfloat16
MESH = pl.DeviceIdType.MESH
NT = (((1,), (1,)), ((), ()))


def probs(rows, some, factor):
    scores = lax.dot_general(rows, some, NT, preferred_element_type=F32)
    peak = jnp.max(scores, axis=0, keepdims=True)
    weights = jnp.exp2((scores - peak) * factor)
    return weights * (1.0 / jnp.sum(weights, axis=0, keepdims=True))


def item_gradient(heads, teacher, student, grads, diff):
    length = teacher.shape[0]
    tw, sw = teacher.shape[1] // heads, student.shape[1] // heads
    x = student[...]
    lane = lax.broadcasted_iota(jnp.int32, x.shape, 1)
    x_t = x.T
    parts = []
    for head in range(heads):
        mine = (lane >= head * sw) & (lane < (head + 1) * sw)
        xh = jnp.where(mine, x, jnp.zeros_like(x))
        th = teacher[:, head * tw : (head + 1) * tw]
        for i in range(0, length, STRIP):
            student_probs = probs(x, xh[i : i + STRIP], LOG2E / math.sqrt(sw))
            teacher_probs = probs(th, th[i : i + STRIP], LOG2E / math.sqrt(tw))
            diff[:, i : i + STRIP] = (student_probs - teacher_probs).astype(BF16)
        xh_t = x_t[head * sw : (head + 1) * sw]
        d = diff[...]
        key_side = lax.dot_general(xh_t, d, NT, preferred_element_type=F32)
        query_side = jnp.dot(xh_t, d, preferred_element_type=F32)
        parts.append(query_side + key_side)
    grads_t = jnp.concatenate(parts, axis=0) * (1.0 / math.sqrt(sw))
    grads[...] = grads_t.T.astype(BF16)


def kernel(ny, nz, heads, teacher_hbm, student_hbm, out, teacher, staged, xs, grads, diff, sems, in_recv, t_sem, level_sem):
    n = ny * nz
    me = lax.axis_index("head")
    y, z = me // nz, me % nz
    items, rows, _ = staged.shape
    width = xs.shape[2]
    load_sem, in_send, out_send, out_recv = (sems.at[i] for i in range(4))

    def peer(t):
        a, dz = t // nz, t % nz
        dy = (a % 2) * ((a + 1) // 2) + (1 - a % 2) * (ny - a // 2)
        return ((y + dy) % ny) * nz + (z + dz) % nz

    load = pltpu.make_async_copy(student_hbm, staged, load_sem)
    load.start()

    def load_teacher(b, _):
        pltpu.make_async_copy(teacher_hbm.at[b], teacher.at[b], t_sem.at[b]).start()
        return 0

    lax.fori_loop(0, items, load_teacher, 0)

    def near(act):
        for step in (1, ny - 1):
            act((y + step) % ny, z)
        pl.when(z > 0)(lambda: act(y, z - 1))
        pl.when(z < nz - 1)(lambda: act(y, z + 1))

    neighbours = 2 + (z > 0).astype(jnp.int32) + (z < nz - 1).astype(jnp.int32)

    my_rows = pl.ds(pl.multiple_of(me * rows, rows), rows)
    my_cols = pl.ds(pl.multiple_of(me * width, width), width)

    def send_in(c, p):
        batch = pl.ds(c * CHUNK, CHUNK)
        pltpu.make_async_remote_copy(
            src_ref=staged.at[batch, :, pl.ds(pl.multiple_of(p * width, width), width)],
            dst_ref=xs.at[batch, my_rows, :],
            send_sem=in_send,
            recv_sem=in_recv.at[c],
            device_id={"head": p},
            device_id_type=MESH,
        ).start()

    def at_distance(c, lo, hi):
        for dy in sorted(range(-((ny - 1) // 2), ny // 2 + 1), key=abs):
            for dz in sorted(range(1 - nz, nz), key=abs):
                if lo <= abs(dy) + abs(dz) <= hi:
                    to = lambda dy=dy, dz=dz: send_in(c, (y + dy + ny) % ny * nz + z + dz)
                    if dz:
                        pl.when((z + dz >= 0) & (z + dz < nz))(to)
                    else:
                        to()

    def all_chunks(lo, hi):
        def one(c, _):
            at_distance(c, lo, hi)
            return 0

        lax.fori_loop(0, items // CHUNK, one, 0)

    barrier = pltpu.get_barrier_semaphore()
    near(lambda yy, zz: pl.semaphore_signal(
        barrier, inc=1, device_id={"head": yy * nz + zz}, device_id_type=MESH
    ))
    load.wait()

    def own(c, _):
        batch = pl.ds(c * CHUNK, CHUNK)
        pltpu.make_async_copy(
            staged.at[batch, :, my_cols], xs.at[batch, my_rows, :], in_recv.at[c]
        ).start()
        return 0

    lax.fori_loop(0, items // CHUNK, own, 0)
    pl.semaphore_wait(barrier, neighbours)
    farthest = ny // 2 + nz - 1
    for level in range(1, farthest + 1):
        if level > 1:
            near(lambda yy, zz: pl.semaphore_signal(
                level_sem.at[level - 2], inc=1, device_id={"head": yy * nz + zz}, device_id_type=MESH
            ))
            pl.semaphore_wait(level_sem.at[level - 2], neighbours)
        if level <= EARLY:
            all_chunks(level, level)
    all_chunks(EARLY + 1, farthest)

    def work(c, _):
        batch = pl.ds(c * CHUNK, CHUNK)
        pltpu.make_async_copy(xs.at[batch], xs.at[batch], in_recv.at[c]).wait()
        for k in range(CHUNK):
            b = c * CHUNK + k
            pltpu.make_async_copy(teacher_hbm.at[b], teacher.at[b], t_sem.at[b]).wait()
            item_gradient(heads, teacher.at[b], xs.at[b], grads.at[b], diff)
        pltpu.make_async_copy(
            grads.at[batch, my_rows, :], out.at[batch, :, my_cols], out_recv
        ).start()

        def to(t, _):
            p = peer(t)
            pltpu.make_async_remote_copy(
                src_ref=grads.at[batch, pl.ds(pl.multiple_of(p * rows, rows), rows), :],
                dst_ref=out.at[batch, :, my_cols],
                send_sem=out_send,
                recv_sem=out_recv,
                device_id={"head": p},
                device_id_type=MESH,
            ).start()
            return 0

        lax.fori_loop(1, n, to, 0)
        return 0

    lax.fori_loop(0, items // CHUNK, work, 0)

    some = pl.ds(0, (n - 1) * rows)
    pltpu.make_async_copy(xs.at[:, some, :], xs.at[:, some, :], in_send).wait()
    pltpu.make_async_copy(grads.at[:, some, :], grads.at[:, some, :], out_send).wait()
    pltpu.make_async_copy(out, out, out_recv).wait()


def solution(mesh):
    n = mesh.shape["head"]
    nz = 4
    heads = RELATION_HEADS // n

    def body(teacher_qkv, student_qkv):
        _, items, length, teacher_width = teacher_qkv.shape
        _, _, rows, student_width = student_qkv.shape
        width = student_width // n
        result = pl.pallas_call(
            functools.partial(kernel, n // nz, nz, heads),
            out_shape=pltpu.VMEM((items, rows, student_width), BF16),
            in_specs=[pl.BlockSpec(memory_space=pl.ANY)] * 2,
            out_specs=pl.BlockSpec(memory_space=pltpu.VMEM),
            scratch_shapes=[
                pltpu.VMEM((items, length, teacher_width), BF16),
                pltpu.VMEM((items, rows, student_width), BF16),
                pltpu.VMEM((items, length, width), BF16),
                pltpu.VMEM((items, length, width), BF16),
                pltpu.VMEM((length, length), BF16),
                pltpu.SemaphoreType.DMA((4,)),
                pltpu.SemaphoreType.DMA((items // CHUNK,)),
                pltpu.SemaphoreType.DMA((items,)),
                pltpu.SemaphoreType.REGULAR((n // nz // 2 + nz - 2,)),
            ],
            compiler_params=pltpu.CompilerParams(
                collective_id=0, has_side_effects=True, vmem_limit_bytes=40 * 2**20
            ),
            name="relation_grads",
        )(*(pltpu.with_memory_space_constraint(a[0], pltpu.HBM) for a in (teacher_qkv, student_qkv)))
        return result[None]

    in_specs = (P(None, ("seq", "batch"), None, "head"), P(None, ("seq", "batch"), "head", None))
    out_specs = P(None, ("seq", "batch"), "head", None)
    return jax.shard_map(body, mesh=mesh, in_specs=in_specs, out_specs=out_specs, check_vma=False)
```

```python
import functools
import math

import jax
import jax.numpy as jnp
from jax import lax
from jax.experimental import pallas as pl
from jax.experimental.pallas import tpu as pltpu
from jax.sharding import PartitionSpec as P

RELATION_HEADS = 64
CHUNK = 2
STRIP = 256
EARLY = 3
LOG2E = 1.4426950408889634
F32, BF16 = jnp.float32, jnp.bfloat16
MESH = pl.DeviceIdType.MESH
NT = (((1,), (1,)), ((), ()))


def probs(rows, some, factor):
    scores = lax.dot_general(rows, some, NT, preferred_element_type=F32)
    peak = jnp.max(scores, axis=0, keepdims=True)
    weights = jnp.exp2((scores - peak) * factor)
    return weights * (1.0 / jnp.sum(weights, axis=0, keepdims=True))


def item_gradient(heads, teacher, student, grads, diff):
    length = teacher.shape[0]
    tw, sw = teacher.shape[1] // heads, student.shape[1] // heads
    x = student[...]
    lane = lax.broadcasted_iota(jnp.int32, x.shape, 1)
    x_t = x.T
    parts = []
    for head in range(heads):
        mine = (lane >= head * sw) & (lane < (head + 1) * sw)
        xh = jnp.where(mine, x, jnp.zeros_like(x))
        th = teacher[:, head * tw : (head + 1) * tw]
        for i in range(0, length, STRIP):
            student_probs = probs(x, xh[i : i + STRIP], LOG2E / math.sqrt(sw))
            teacher_probs = probs(th, th[i : i + STRIP], LOG2E / math.sqrt(tw))
            diff[:, i : i + STRIP] = (student_probs - teacher_probs).astype(BF16)
        xh_t = x_t[head * sw : (head + 1) * sw]
        d = diff[...]
        key_side = lax.dot_general(xh_t, d, NT, preferred_element_type=F32)
        query_side = jnp.dot(xh_t, d, preferred_element_type=F32)
        parts.append(query_side + key_side)
    grads_t = jnp.concatenate(parts, axis=0) * (1.0 / math.sqrt(sw))
    grads[...] = grads_t.T.astype(BF16)


def kernel(ny, nz, heads, teacher_hbm, student_hbm, out, teacher, xs, grads, diff, sems, in_recv, t_sem, level_sem):
    n = ny * nz
    me = lax.axis_index("head")
    y, z = me // nz, me % nz
    items, rows, _ = student_hbm.shape
    width = xs.shape[2]
    in_send, out_send, out_recv = (sems.at[i] for i in range(3))

    def load_teacher(b, _):
        pltpu.make_async_copy(teacher_hbm.at[b], teacher.at[b], t_sem.at[b]).start()
        return 0

    lax.fori_loop(0, items, load_teacher, 0)

    def near(act):
        for step in (1, ny - 1):
            act((y + step) % ny, z)
        pl.when(z > 0)(lambda: act(y, z - 1))
        pl.when(z < nz - 1)(lambda: act(y, z + 1))

    neighbours = 2 + (z > 0).astype(jnp.int32) + (z < nz - 1).astype(jnp.int32)

    my_rows = pl.ds(pl.multiple_of(me * rows, rows), rows)
    my_cols = pl.ds(pl.multiple_of(me * width, width), width)

    def send_in(c, p):
        batch = pl.ds(c * CHUNK, CHUNK)
        pltpu.make_async_remote_copy(
            src_ref=student_hbm.at[batch, :, pl.ds(pl.multiple_of(p * width, width), width)],
            dst_ref=xs.at[batch, my_rows, :],
            send_sem=in_send,
            recv_sem=in_recv.at[c],
            device_id={"head": p},
            device_id_type=MESH,
        ).start()

    def peers(send, lo, hi):
        for dy in sorted(range(-((ny - 1) // 2), ny // 2 + 1), key=abs):
            for dz in sorted(range(1 - nz, nz), key=abs):
                if lo <= abs(dy) + abs(dz) <= hi:
                    to = lambda dy=dy, dz=dz: send((y + dy + ny) % ny * nz + z + dz)
                    if dz:
                        pl.when((z + dz >= 0) & (z + dz < nz))(to)
                    else:
                        to()

    def all_chunks(lo, hi):
        def one(c, _):
            peers(lambda p: send_in(c, p), lo, hi)
            return 0

        lax.fori_loop(0, items // CHUNK, one, 0)

    barrier = pltpu.get_barrier_semaphore()
    near(lambda yy, zz: pl.semaphore_signal(
        barrier, inc=1, device_id={"head": yy * nz + zz}, device_id_type=MESH
    ))

    def own(c, _):
        batch = pl.ds(c * CHUNK, CHUNK)
        pltpu.make_async_copy(
            student_hbm.at[batch, :, my_cols], xs.at[batch, my_rows, :], in_recv.at[c]
        ).start()
        return 0

    lax.fori_loop(0, items // CHUNK, own, 0)
    pl.semaphore_wait(barrier, neighbours)
    farthest = ny // 2 + nz - 1
    for level in range(1, farthest + 1):
        if level > 1:
            pl.semaphore_wait(level_sem.at[level - 2], neighbours)
        if level < farthest:
            near(lambda yy, zz: pl.semaphore_signal(
                level_sem.at[level - 1], inc=1, device_id={"head": yy * nz + zz}, device_id_type=MESH
            ))
        if level <= EARLY:
            all_chunks(level, level)
    all_chunks(EARLY + 1, farthest)

    def work(c, _):
        batch = pl.ds(c * CHUNK, CHUNK)
        pltpu.make_async_copy(xs.at[batch], xs.at[batch], in_recv.at[c]).wait()
        for k in range(CHUNK):
            b = c * CHUNK + k
            pltpu.make_async_copy(teacher_hbm.at[b], teacher.at[b], t_sem.at[b]).wait()
            item_gradient(heads, teacher.at[b], xs.at[b], grads.at[b], diff)
        pltpu.make_async_copy(
            grads.at[batch, my_rows, :], out.at[batch, :, my_cols], out_recv
        ).start()

        def send_out(p):
            pltpu.make_async_remote_copy(
                src_ref=grads.at[batch, pl.ds(pl.multiple_of(p * rows, rows), rows), :],
                dst_ref=out.at[batch, :, my_cols],
                send_sem=out_send,
                recv_sem=out_recv,
                device_id={"head": p},
                device_id_type=MESH,
            ).start()

        last = items // CHUNK - 1
        pl.when(c < last)(lambda: peers(send_out, 1, farthest))

        @pl.when(c == last)
        def _():
            for hops in range(farthest, 0, -1):
                peers(send_out, hops, hops)

        return 0

    lax.fori_loop(0, items // CHUNK, work, 0)

    some = pl.ds(0, (n - 1) * rows)
    pltpu.make_async_copy(xs.at[:, some, :], xs.at[:, some, :], in_send).wait()
    pltpu.make_async_copy(grads.at[:, some, :], grads.at[:, some, :], out_send).wait()
    pltpu.make_async_copy(out, out, out_recv).wait()


def solution(mesh):
    n = mesh.shape["head"]
    nz = 4
    heads = RELATION_HEADS // n

    def body(teacher_qkv, student_qkv):
        _, items, length, teacher_width = teacher_qkv.shape
        _, _, rows, student_width = student_qkv.shape
        width = student_width // n
        result = pl.pallas_call(
            functools.partial(kernel, n // nz, nz, heads),
            out_shape=pltpu.VMEM((items, rows, student_width), BF16),
            in_specs=[pl.BlockSpec(memory_space=pl.ANY)] * 2,
            out_specs=pl.BlockSpec(memory_space=pltpu.VMEM),
            scratch_shapes=[
                pltpu.VMEM((items, length, teacher_width), BF16),
                pltpu.VMEM((items, length, width), BF16),
                pltpu.VMEM((items, length, width), BF16),
                pltpu.VMEM((length, length), BF16),
                pltpu.SemaphoreType.DMA((3,)),
                pltpu.SemaphoreType.DMA((items // CHUNK,)),
                pltpu.SemaphoreType.DMA((items,)),
                pltpu.SemaphoreType.REGULAR((n // nz // 2 + nz - 2,)),
            ],
            compiler_params=pltpu.CompilerParams(
                collective_id=0, has_side_effects=True, vmem_limit_bytes=40 * 2**20
            ),
            name="relation_grads",
        )(*(pltpu.with_memory_space_constraint(a[0], pltpu.HBM) for a in (teacher_qkv, student_qkv)))
        return result[None]

    in_specs = (P(None, ("seq", "batch"), None, "head"), P(None, ("seq", "batch"), "head", None))
    out_specs = P(None, ("seq", "batch"), "head", None)
    return jax.shard_map(body, mesh=mesh, in_specs=in_specs, out_specs=out_specs, check_vma=False)
```

```python
import functools
import math

import jax
import jax.numpy as jnp
from jax import lax
from jax.experimental import pallas as pl
from jax.experimental.pallas import tpu as pltpu
from jax.sharding import PartitionSpec as P

RELATION_HEADS = 64
CHUNK = 2
STRIP = 256
EARLY = 3
LOG2E = 1.4426950408889634
F32, BF16 = jnp.float32, jnp.bfloat16
MESH = pl.DeviceIdType.MESH
NT = (((1,), (1,)), ((), ()))


def probs(rows, some, factor):
    scores = lax.dot_general(rows, some, NT, preferred_element_type=F32)
    peak = jnp.max(scores, axis=0, keepdims=True)
    weights = jnp.exp2((scores - peak) * factor)
    return weights * (1.0 / jnp.sum(weights, axis=0, keepdims=True))


def teacher_side(heads, teacher, known):
    length = teacher.shape[0]
    tw = teacher.shape[1] // heads
    for head in range(heads):
        th = teacher[:, head * tw : (head + 1) * tw]
        for i in range(0, length, STRIP):
            known[head, :, i : i + STRIP] = probs(th, th[i : i + STRIP], LOG2E / math.sqrt(tw))


def item_gradient(heads, known, student, grads, diff):
    length = student.shape[0]
    sw = student.shape[1] // heads
    x = student[...]
    lane = lax.broadcasted_iota(jnp.int32, x.shape, 1)
    x_t = x.T
    parts = []
    for head in range(heads):
        mine = (lane >= head * sw) & (lane < (head + 1) * sw)
        xh = jnp.where(mine, x, jnp.zeros_like(x))
        for i in range(0, length, STRIP):
            student_probs = probs(x, xh[i : i + STRIP], LOG2E / math.sqrt(sw))
            diff[:, i : i + STRIP] = (student_probs - known[head, :, i : i + STRIP]).astype(BF16)
        xh_t = x_t[head * sw : (head + 1) * sw]
        d = diff[...]
        key_side = lax.dot_general(xh_t, d, NT, preferred_element_type=F32)
        query_side = jnp.dot(xh_t, d, preferred_element_type=F32)
        parts.append(query_side + key_side)
    grads_t = jnp.concatenate(parts, axis=0) * (1.0 / math.sqrt(sw))
    grads[...] = grads_t.T.astype(BF16)


def kernel(ny, nz, heads, teacher_hbm, student_hbm, out, teacher, xs, grads, known, diff, sems, in_recv, t_sem, level_sem):
    n = ny * nz
    me = lax.axis_index("head")
    y, z = me // nz, me % nz
    items, rows, _ = student_hbm.shape
    width = xs.shape[2]
    in_send, out_send, out_recv = (sems.at[i] for i in range(3))

    def load_teacher(b, _):
        pltpu.make_async_copy(teacher_hbm.at[b], teacher.at[b], t_sem.at[b]).start()
        return 0

    lax.fori_loop(0, items, load_teacher, 0)

    def near(act):
        for step in (1, ny - 1):
            act((y + step) % ny, z)
        pl.when(z > 0)(lambda: act(y, z - 1))
        pl.when(z < nz - 1)(lambda: act(y, z + 1))

    neighbours = 2 + (z > 0).astype(jnp.int32) + (z < nz - 1).astype(jnp.int32)

    my_rows = pl.ds(pl.multiple_of(me * rows, rows), rows)
    my_cols = pl.ds(pl.multiple_of(me * width, width), width)

    def send_in(c, p):
        batch = pl.ds(c * CHUNK, CHUNK)
        pltpu.make_async_remote_copy(
            src_ref=student_hbm.at[batch, :, pl.ds(pl.multiple_of(p * width, width), width)],
            dst_ref=xs.at[batch, my_rows, :],
            send_sem=in_send,
            recv_sem=in_recv.at[c],
            device_id={"head": p},
            device_id_type=MESH,
        ).start()

    def peers(send, lo, hi):
        for dy in sorted(range(-((ny - 1) // 2), ny // 2 + 1), key=abs):
            for dz in sorted(range(1 - nz, nz), key=abs):
                if lo <= abs(dy) + abs(dz) <= hi:
                    to = lambda dy=dy, dz=dz: send((y + dy + ny) % ny * nz + z + dz)
                    if dz:
                        pl.when((z + dz >= 0) & (z + dz < nz))(to)
                    else:
                        to()

    def all_chunks(lo, hi):
        def one(c, _):
            peers(lambda p: send_in(c, p), lo, hi)
            return 0

        lax.fori_loop(0, items // CHUNK, one, 0)

    barrier = pltpu.get_barrier_semaphore()
    near(lambda yy, zz: pl.semaphore_signal(
        barrier, inc=1, device_id={"head": yy * nz + zz}, device_id_type=MESH
    ))

    def own(c, _):
        batch = pl.ds(c * CHUNK, CHUNK)
        pltpu.make_async_copy(
            student_hbm.at[batch, :, my_cols], xs.at[batch, my_rows, :], in_recv.at[c]
        ).start()
        return 0

    lax.fori_loop(0, items // CHUNK, own, 0)
    pl.semaphore_wait(barrier, neighbours)
    farthest = ny // 2 + nz - 1
    for level in range(1, farthest + 1):
        if level > 1:
            pl.semaphore_wait(level_sem.at[level - 2], neighbours)
        if level < farthest:
            near(lambda yy, zz: pl.semaphore_signal(
                level_sem.at[level - 1], inc=1, device_id={"head": yy * nz + zz}, device_id_type=MESH
            ))
        if level <= EARLY:
            all_chunks(level, level)
    all_chunks(EARLY + 1, farthest)

    def ahead(b, _):
        pltpu.make_async_copy(teacher_hbm.at[b], teacher.at[b], t_sem.at[b]).wait()
        teacher_side(heads, teacher.at[b], known.at[b])
        return 0

    lax.fori_loop(0, items, ahead, 0)

    def work(c, _):
        batch = pl.ds(c * CHUNK, CHUNK)
        pltpu.make_async_copy(xs.at[batch], xs.at[batch], in_recv.at[c]).wait()
        for k in range(CHUNK):
            b = c * CHUNK + k
            item_gradient(heads, known.at[b], xs.at[b], grads.at[b], diff)
        pltpu.make_async_copy(
            grads.at[batch, my_rows, :], out.at[batch, :, my_cols], out_recv
        ).start()

        def send_out(p):
            pltpu.make_async_remote_copy(
                src_ref=grads.at[batch, pl.ds(pl.multiple_of(p * rows, rows), rows), :],
                dst_ref=out.at[batch, :, my_cols],
                send_sem=out_send,
                recv_sem=out_recv,
                device_id={"head": p},
                device_id_type=MESH,
            ).start()

        last = items // CHUNK - 1
        pl.when(c < last)(lambda: peers(send_out, 1, farthest))

        @pl.when(c == last)
        def _():
            for hops in range(farthest, 0, -1):
                peers(send_out, hops, hops)

        return 0

    lax.fori_loop(0, items // CHUNK, work, 0)

    some = pl.ds(0, (n - 1) * rows)
    pltpu.make_async_copy(xs.at[:, some, :], xs.at[:, some, :], in_send).wait()
    pltpu.make_async_copy(grads.at[:, some, :], grads.at[:, some, :], out_send).wait()
    pltpu.make_async_copy(out, out, out_recv).wait()


def solution(mesh):
    n = mesh.shape["head"]
    nz = 4
    heads = RELATION_HEADS // n

    def body(teacher_qkv, student_qkv):
        _, items, length, teacher_width = teacher_qkv.shape
        _, _, rows, student_width = student_qkv.shape
        width = student_width // n
        result = pl.pallas_call(
            functools.partial(kernel, n // nz, nz, heads),
            out_shape=pltpu.VMEM((items, rows, student_width), BF16),
            in_specs=[pl.BlockSpec(memory_space=pl.ANY)] * 2,
            out_specs=pl.BlockSpec(memory_space=pltpu.VMEM),
            scratch_shapes=[
                pltpu.VMEM((items, length, teacher_width), BF16),
                pltpu.VMEM((items, length, width), BF16),
                pltpu.VMEM((items, length, width), BF16),
                pltpu.VMEM((items, heads, length, length), F32),
                pltpu.VMEM((length, length), BF16),
                pltpu.SemaphoreType.DMA((3,)),
                pltpu.SemaphoreType.DMA((items // CHUNK,)),
                pltpu.SemaphoreType.DMA((items,)),
                pltpu.SemaphoreType.REGULAR((n // nz // 2 + nz - 2,)),
            ],
            compiler_params=pltpu.CompilerParams(
                collective_id=0, has_side_effects=True, vmem_limit_bytes=40 * 2**20
            ),
            name="relation_grads",
        )(*(pltpu.with_memory_space_constraint(a[0], pltpu.HBM) for a in (teacher_qkv, student_qkv)))
        return result[None]

    in_specs = (P(None, ("seq", "batch"), None, "head"), P(None, ("seq", "batch"), "head", None))
    out_specs = P(None, ("seq", "batch"), "head", None)
    return jax.shard_map(body, mesh=mesh, in_specs=in_specs, out_specs=out_specs, check_vma=False)
```

```python
import functools
import math

import jax
import jax.numpy as jnp
from jax import lax
from jax.experimental import pallas as pl
from jax.experimental.pallas import tpu as pltpu
from jax.sharding import PartitionSpec as P

RELATION_HEADS = 64
CHUNK = 2
STRIP = 256
EARLY = 3
LOG2E = 1.4426950408889634
F32, BF16 = jnp.float32, jnp.bfloat16
MESH = pl.DeviceIdType.MESH
NT = (((1,), (1,)), ((), ()))


def probs(rows, some, factor):
    scores = lax.dot_general(rows, some, NT, preferred_element_type=F32)
    peak = jnp.max(scores, axis=0, keepdims=True)
    weights = jnp.exp2((scores - peak) * factor)
    return weights * (1.0 / jnp.sum(weights, axis=0, keepdims=True))


def teacher_side(heads, teacher, known):
    length = teacher.shape[0]
    tw = teacher.shape[1] // heads
    for head in range(heads):
        th = teacher[:, head * tw : (head + 1) * tw]
        for i in range(0, length, STRIP):
            known[head, :, i : i + STRIP] = probs(th, th[i : i + STRIP], LOG2E / math.sqrt(tw))


def item_gradient(heads, known, student, grads, diff):
    length = student.shape[0]
    sw = student.shape[1] // heads
    x = student[...]
    lane = lax.broadcasted_iota(jnp.int32, x.shape, 1)
    x_t = x.T
    parts = []
    for head in range(heads):
        mine = (lane >= head * sw) & (lane < (head + 1) * sw)
        xh = jnp.where(mine, x, jnp.zeros_like(x))
        for i in range(0, length, STRIP):
            student_probs = probs(x, xh[i : i + STRIP], LOG2E / math.sqrt(sw))
            diff[:, i : i + STRIP] = (student_probs - known[head, :, i : i + STRIP]).astype(BF16)
        xh_t = x_t[head * sw : (head + 1) * sw]
        d = diff[...]
        key_side = lax.dot_general(xh_t, d, NT, preferred_element_type=F32)
        query_side = jnp.dot(xh_t, d, preferred_element_type=F32)
        parts.append(query_side + key_side)
    grads_t = jnp.concatenate(parts, axis=0) * (1.0 / math.sqrt(sw))
    grads[...] = grads_t.T.astype(BF16)


def kernel(ny, nz, heads, teacher_hbm, student_hbm, out, teacher, xs, grads, known, diff, sems, in_recv, t_sem, level_sem):
    n = ny * nz
    me = lax.axis_index("head")
    y, z = me // nz, me % nz
    items, rows, _ = student_hbm.shape
    width = xs.shape[2]
    in_send, out_send, out_recv = (sems.at[i] for i in range(3))

    def load_teacher(b, _):
        pltpu.make_async_copy(teacher_hbm.at[b], teacher.at[b], t_sem.at[b]).start()
        return 0

    def near(act):
        for step in (1, ny - 1):
            act((y + step) % ny, z)
        pl.when(z > 0)(lambda: act(y, z - 1))
        pl.when(z < nz - 1)(lambda: act(y, z + 1))

    neighbours = 2 + (z > 0).astype(jnp.int32) + (z < nz - 1).astype(jnp.int32)

    my_rows = pl.ds(pl.multiple_of(me * rows, rows), rows)
    my_cols = pl.ds(pl.multiple_of(me * width, width), width)

    def send_in(c, p):
        batch = pl.ds(c * CHUNK, CHUNK)
        pltpu.make_async_remote_copy(
            src_ref=student_hbm.at[batch, :, pl.ds(pl.multiple_of(p * width, width), width)],
            dst_ref=xs.at[batch, my_rows, :],
            send_sem=in_send,
            recv_sem=in_recv.at[c],
            device_id={"head": p},
            device_id_type=MESH,
        ).start()

    def peers(send, lo, hi):
        for dy in sorted(range(-((ny - 1) // 2), ny // 2 + 1), key=abs):
            for dz in sorted(range(1 - nz, nz), key=abs):
                if lo <= abs(dy) + abs(dz) <= hi:
                    to = lambda dy=dy, dz=dz: send((y + dy + ny) % ny * nz + z + dz)
                    if dz:
                        pl.when((z + dz >= 0) & (z + dz < nz))(to)
                    else:
                        to()

    def all_chunks(lo, hi):
        def one(c, _):
            peers(lambda p: send_in(c, p), lo, hi)
            return 0

        lax.fori_loop(0, items // CHUNK, one, 0)

    barrier = pltpu.get_barrier_semaphore()
    near(lambda yy, zz: pl.semaphore_signal(
        barrier, inc=1, device_id={"head": yy * nz + zz}, device_id_type=MESH
    ))

    lax.fori_loop(0, items, load_teacher, 0)

    def own(c, _):
        batch = pl.ds(c * CHUNK, CHUNK)
        pltpu.make_async_copy(
            student_hbm.at[batch, :, my_cols], xs.at[batch, my_rows, :], in_recv.at[c]
        ).start()
        return 0

    lax.fori_loop(0, items // CHUNK, own, 0)
    pl.semaphore_wait(barrier, neighbours)
    farthest = ny // 2 + nz - 1
    for level in range(1, farthest + 1):
        if level > 1:
            pl.semaphore_wait(level_sem.at[level - 2], neighbours)
        if level < farthest:
            near(lambda yy, zz: pl.semaphore_signal(
                level_sem.at[level - 1], inc=1, device_id={"head": yy * nz + zz}, device_id_type=MESH
            ))
        if level <= EARLY:
            all_chunks(level, level)
    all_chunks(EARLY + 1, farthest)

    def ahead(b, _):
        pltpu.make_async_copy(teacher_hbm.at[b], teacher.at[b], t_sem.at[b]).wait()
        teacher_side(heads, teacher.at[b], known.at[b])
        return 0

    lax.fori_loop(0, items, ahead, 0)

    def work(c, _):
        batch = pl.ds(c * CHUNK, CHUNK)
        pltpu.make_async_copy(xs.at[batch], xs.at[batch], in_recv.at[c]).wait()
        for k in range(CHUNK):
            b = c * CHUNK + k
            item_gradient(heads, known.at[b], xs.at[b], grads.at[b], diff)
        pltpu.make_async_copy(
            grads.at[batch, my_rows, :], out.at[batch, :, my_cols], out_recv
        ).start()

        def send_out(p):
            pltpu.make_async_remote_copy(
                src_ref=grads.at[batch, pl.ds(pl.multiple_of(p * rows, rows), rows), :],
                dst_ref=out.at[batch, :, my_cols],
                send_sem=out_send,
                recv_sem=out_recv,
                device_id={"head": p},
                device_id_type=MESH,
            ).start()

        last = items // CHUNK - 1
        pl.when(c < last)(lambda: peers(send_out, 1, farthest))

        @pl.when(c == last)
        def _():
            ways = [(dy, dz) for dy in range(-((ny - 1) // 2), ny // 2 + 1) for dz in range(1 - nz, nz) if dy or dz]
            for dy, dz in sorted(ways, key=lambda way: 1.5 * way[1] - abs(way[0]) - abs(way[1])):
                to = lambda dy=dy, dz=dz: send_out((y + dy + ny) % ny * nz + z + dz)
                pl.when((z + dz >= 0) & (z + dz < nz))(to)

        return 0

    lax.fori_loop(0, items // CHUNK, work, 0)

    some = pl.ds(0, (n - 1) * rows)
    pltpu.make_async_copy(xs.at[:, some, :], xs.at[:, some, :], in_send).wait()
    pltpu.make_async_copy(grads.at[:, some, :], grads.at[:, some, :], out_send).wait()
    pltpu.make_async_copy(out, out, out_recv).wait()


def solution(mesh):
    n = mesh.shape["head"]
    nz = 4
    heads = RELATION_HEADS // n

    def body(teacher_qkv, student_qkv):
        _, items, length, teacher_width = teacher_qkv.shape
        _, _, rows, student_width = student_qkv.shape
        width = student_width // n
        result = pl.pallas_call(
            functools.partial(kernel, n // nz, nz, heads),
            out_shape=pltpu.VMEM((items, rows, student_width), BF16),
            in_specs=[pl.BlockSpec(memory_space=pl.ANY)] * 2,
            out_specs=pl.BlockSpec(memory_space=pltpu.VMEM),
            scratch_shapes=[
                pltpu.VMEM((items, length, teacher_width), BF16),
                pltpu.VMEM((items, length, width), BF16),
                pltpu.VMEM((items, length, width), BF16),
                pltpu.VMEM((items, heads, length, length), F32),
                pltpu.VMEM((length, length), BF16),
                pltpu.SemaphoreType.DMA((3,)),
                pltpu.SemaphoreType.DMA((items // CHUNK,)),
                pltpu.SemaphoreType.DMA((items,)),
                pltpu.SemaphoreType.REGULAR((n // nz // 2 + nz - 2,)),
            ],
            compiler_params=pltpu.CompilerParams(
                collective_id=0, has_side_effects=True, vmem_limit_bytes=40 * 2**20
            ),
            name="relation_grads",
        )(*(pltpu.with_memory_space_constraint(a[0], pltpu.HBM) for a in (teacher_qkv, student_qkv)))
        return result[None]

    in_specs = (P(None, ("seq", "batch"), None, "head"), P(None, ("seq", "batch"), "head", None))
    out_specs = P(None, ("seq", "batch"), "head", None)
    return jax.shard_map(body, mesh=mesh, in_specs=in_specs, out_specs=out_specs, check_vma=False)
```
